32 devices in a mesh: sp: 8 (over z, core), fsdp: 4 (over y, x).
Axes of the slice: x: 2, y: 2, z: 4, core: 2. Of those that a mesh axis runs over, the one named last changes fastest.
Arguments:
- hidden_in: bfloat16 [4, 2048, 1024], P('fsdp', 'sp'), may hold values from -6 to 6
- positions: int32 [4, 2048], P('fsdp', 'sp'), may hold values from 0 to 2047, as said below
- out_cotangent: bfloat16 [4, 2048, 1024], P('fsdp', 'sp'), may hold values from -6 to 6
- attn_gain: bfloat16 [1024], P('fsdp'), may hold values from 0.099609375 to 1.8984375
- attn_shift: bfloat16 [1024], P('fsdp'), may hold values from -3 to 3
- mlp_gain: bfloat16 [1024], P('fsdp'), may hold values from 0.099609375 to 1.8984375
- mlp_shift: bfloat16 [1024], P('fsdp'), may hold values from -3 to 3
- qkv_weight: bfloat16 [1024, 3072], P('fsdp')
- qkv_bias: bfloat16 [3072], P('fsdp'), may hold values from -3 to 3
- dense_weight: bfloat16 [1024, 1024], P('fsdp'), may hold values from -1.5 to 1.5
- dense_bias: bfloat16 [1024], P('fsdp'), may hold values from -3 to 3
- up_weight: bfloat16 [1024, 4096], P('fsdp'), may hold values from -0.1875 to 0.1875
- up_bias: bfloat16 [4096], P('fsdp'), may hold values from -3 to 3
- down_weight: bfloat16 [4096, 1024], P('fsdp'), may hold values from -0.09375 to 0.09375
- down_bias: bfloat16 [1024], P('fsdp'), may hold values from -3 to 3
Outputs:
- block_out: bfloat16 [4, 2048, 1024], P('fsdp', 'sp')
- input_grad: float32 [4, 2048, 1024], P('fsdp', 'sp')
- attn_gain_grad: float32 [1024], P(('sp', 'fsdp'))
- attn_shift_grad: float32 [1024], P(('sp', 'fsdp'))
- mlp_gain_grad: float32 [1024], P(('sp', 'fsdp'))
- mlp_shift_grad: float32 [1024], P(('sp', 'fsdp'))
- qkv_weight_grad: float32 [1024, 3072], P(('sp', 'fsdp'))
- qkv_bias_grad: float32 [3072], P(('sp', 'fsdp'))
- dense_weight_grad: float32 [1024, 1024], P(('sp', 'fsdp'))
- dense_bias_grad: float32 [1024], P(('sp', 'fsdp'))
- up_weight_grad: float32 [1024, 4096], P(('sp', 'fsdp'))
- up_bias_grad: float32 [4096], P(('sp', 'fsdp'))
- down_weight_grad: float32 [4096, 1024], P(('sp', 'fsdp'))
- down_bias_grad: float32 [1024], P(('sp', 'fsdp'))
The draws below stay inside these ranges and needn't reach their ends.
Inputs may be any that keep to these rules, and one draw needn't show every extreme that they name: Each sequence is a pack of whole documents: a token's position is its distance to its document's first token, so positions are 0 where a document begins and rise by one per token inside a document; every sequence begins a document.
All inputs are finite; a program needn't handle non-finite values.
Results may differ from the reference program's by a relative error of at most 0.011.
Values may be sent and summed in bfloat16 or wider, within the bound.
A program may use at most 256 MiB of HBM per device.

```python
import math
import jax
import jax.numpy as jnp
from jax import lax

D = 1024
HEADS = 16
HD = 64
ROT = 16
FF = 4096
SEQ_LEN = 2048
SEQS_ALL = 4


def draw_qkv_weight(key, part):
    weights_all = jax.random.normal(jax.random.fold_in(key, 11), (D, HEADS, 3, HD), jnp.float32) * D ** (-0.5)
    return weights_all.reshape(D, 3 * D).astype(jnp.bfloat16)


def draw_positions(key, part):
    grid_shape = (SEQS_ALL, SEQ_LEN)
    breaks = jax.random.randint(jax.random.fold_in(key, 21), grid_shape, 0, SEQ_LEN) < 4
    column = jnp.arange(SEQ_LEN, dtype=jnp.int32)[None, :]
    first_row = jnp.arange(SEQS_ALL, dtype=jnp.int32)[:, None] == 0
    breaks = breaks & jnp.logical_not(first_row) | (column == 0)
    starts = lax.cummax(jnp.where(breaks, column, 0), axis=1)
    return (column - starts).astype(jnp.int32)


def shard_levels(rng, dims, shards, least, top_value):
    def one(axis_at, blocks):
        steps = jax.random.uniform(jax.random.fold_in(jax.random.fold_in(rng, 6), axis_at), (blocks,), jnp.float32, least / len(shards), top_value / len(shards))
        return jnp.repeat(jnp.exp(steps), dims[axis_at] // blocks).reshape((-1,) + (1,) * (len(dims) - axis_at - 1))

    loudness = one(*shards[0])
    for cut in shards[1:]:
        loudness = loudness * one(*cut)
    return loudness


def noise(key, extent, deviation, bound, cuts=(), held_as=jnp.bfloat16):
    drawn = jax.random.normal(key, extent, jnp.float32) * deviation
    if len(cuts) > 0:
        drawn = shard_levels(key, extent, cuts, -0.22, 0.18) * drawn
    return jnp.clip(drawn, min=-bound, max=bound).astype(held_as)


def setup_inputs(seed: int = 0) -> dict:
    arg_keys = jax.random.split(jax.random.key(seed), 16)
    hidden_in = noise(arg_keys[0], (SEQS_ALL, SEQ_LEN, D), 1.0, 6.0, ((0, 4), (1, 8)))
    positions = draw_positions(jax.random.fold_in(arg_keys[15], 71), 0)
    out_cotangent = noise(arg_keys[2], (SEQS_ALL, SEQ_LEN, D), 1.0, 6.0, ((0, 4), (1, 8)))
    attn_gain = jnp.clip(1.0 + 0.18 * jax.random.normal(arg_keys[3], (D,), jnp.float32), 0.099609375, 1.8984375).astype(jnp.bfloat16)
    attn_shift = noise(arg_keys[4], (D,), 0.5, 3.0, ((0, 4),))
    mlp_gain = jnp.clip(1.0 + 0.18 * jax.random.normal(arg_keys[5], (D,), jnp.float32), 0.099609375, 1.8984375).astype(jnp.bfloat16)
    mlp_shift = noise(arg_keys[6], (D,), 0.5, 3.0, ((0, 4),))
    qkv_weight = draw_qkv_weight(jax.random.fold_in(arg_keys[15], 71), 0)
    qkv_bias = noise(arg_keys[8], (3 * D,), 0.5, 3.0, ((0, 4),))
    dense_weight = noise(arg_keys[9], (D, D), (D // 64) ** -0.5, 1.5, ((0, 4),))
    dense_bias = noise(arg_keys[10], (D,), 0.5, 3.0, ((0, 4),))
    up_weight = noise(arg_keys[11], (D, FF), D ** -0.5, 0.1875, ((0, 4),))
    up_bias = noise(arg_keys[12], (FF,), 0.5, 3.0, ((0, 4),))
    down_weight = noise(arg_keys[13], (FF, D), FF ** -0.5, 0.09375, ((0, 4),))
    down_bias = noise(arg_keys[14], (D,), 0.5, 3.0, ((0, 4),))
    return {"hidden_in": hidden_in, "positions": positions, "out_cotangent": out_cotangent, "attn_gain": attn_gain, "attn_shift": attn_shift, "mlp_gain": mlp_gain, "mlp_shift": mlp_shift, "qkv_weight": qkv_weight, "qkv_bias": qkv_bias, "dense_weight": dense_weight, "dense_bias": dense_bias, "up_weight": up_weight, "up_bias": up_bias, "down_weight": down_weight, "down_bias": down_bias}


NORM_EPS = 1e-05
ROPE_BASE = 10000.0
ROOT_HALF = 0.7071067811865476
INV_ROOT_TWO_PI = 0.3989422804014327
MASK_FILL = -1e+30

def layer_norm(values):
    row_mean = lax.optimization_barrier(jnp.mean(values, axis=-1, keepdims=True))
    centered = values - row_mean
    inv_std = lax.rsqrt(lax.optimization_barrier(jnp.mean(centered * centered, axis=-1, keepdims=True)) + NORM_EPS)
    return (centered * inv_std, inv_std)

def affine(normed, norm_gain, norm_shift):
    return normed * norm_gain.astype(jnp.float32) + norm_shift.astype(jnp.float32)

def norm_backward(grad_out, normed, inv_std, norm_gain):
    grad_normed = grad_out * norm_gain.astype(jnp.float32)
    mean_grad = lax.optimization_barrier(jnp.mean(grad_normed, axis=-1, keepdims=True))
    mean_cross = lax.optimization_barrier(jnp.mean(grad_normed * normed, axis=-1, keepdims=True))
    return inv_std * (grad_normed - mean_grad - normed * mean_cross)

def gelu_pair(hidden):
    cdf_part = 0.5 * (1.0 + jax.scipy.special.erf(hidden * ROOT_HALF))
    density = jnp.exp(-0.5 * hidden * hidden) * INV_ROOT_TWO_PI
    return (hidden * cdf_part, cdf_part + hidden * density)

def rope_tables(positions, rot_dims):
    half_dims = rot_dims // 2
    inv_freq = jnp.exp(jnp.arange(half_dims, dtype=jnp.float32) * (-2.0 * math.log(ROPE_BASE) / rot_dims))
    angles = positions.astype(jnp.float32)[..., None] * inv_freq
    angles = jnp.concatenate([angles, angles], axis=-1)
    return (jnp.cos(angles), jnp.sin(angles))

def rotate(values, cosine, sine_table, rot_dims):
    half_dims = rot_dims // 2
    leading = values[..., :rot_dims]
    turned = jnp.concatenate([-leading[..., half_dims:], leading[..., :half_dims]], axis=-1)
    leading = leading * cosine[..., None, :] + turned * sine_table[..., None, :]
    return jnp.concatenate([leading, values[..., rot_dims:]], axis=-1)

def rotate_back(grad_values, cosine, sine_table, rot_dims):
    half_dims = rot_dims // 2
    leading = grad_values[..., :rot_dims]
    scaled = leading * sine_table[..., None, :]
    leading = leading * cosine[..., None, :] + jnp.concatenate([scaled[..., half_dims:], -scaled[..., :half_dims]], axis=-1)
    return jnp.concatenate([leading, grad_values[..., rot_dims:]], axis=-1)

def reference(hidden_in, positions, out_cotangent, attn_gain, attn_shift, mlp_gain, mlp_shift, qkv_weight, qkv_bias, dense_weight, dense_bias, up_weight, up_bias, down_weight, down_bias):
    scale_value = 1.0 / math.sqrt(HD)
    length = SEQ_LEN

    def one_sequence(running, inputs):
        tokens_seq, pos_seq, cot_seq = inputs
        x_full = tokens_seq.astype(jnp.float32)
        normed, inv_std = layer_norm(x_full)
        attn_in = affine(normed, attn_gain, attn_shift).astype(jnp.bfloat16)
        mlp_in = affine(normed, mlp_gain, mlp_shift).astype(jnp.bfloat16)
        joined = jnp.dot(attn_in, qkv_weight, preferred_element_type=jnp.float32) + qkv_bias.astype(jnp.float32)
        joined = joined.reshape(length, HEADS, 3, HD)
        cosine, sine_table = rope_tables(pos_seq, ROT)
        query_all = rotate(joined[:, :, 0], cosine, sine_table, ROT).astype(jnp.bfloat16).transpose(1, 0, 2)
        key_all = rotate(joined[:, :, 1], cosine, sine_table, ROT).astype(jnp.bfloat16).transpose(1, 0, 2)
        value_all = joined[:, :, 2].astype(jnp.bfloat16).transpose(1, 0, 2)
        row_index = jnp.arange(length, dtype=jnp.int32)
        doc_start = row_index - pos_seq.astype(jnp.int32)
        allowed = (row_index[None, :] <= row_index[:, None]) & (row_index[None, :] >= doc_start[:, None])

        def masked_scores(query_rows, key_rows):
            scores = jnp.dot(query_rows, key_rows.T, preferred_element_type=jnp.float32) * scale_value
            return jnp.where(allowed, scores, MASK_FILL)

        def head_forward(operands):
            query_rows, key_rows, value_rows = operands
            scores = masked_scores(query_rows, key_rows)
            row_max = lax.optimization_barrier(jnp.max(scores, axis=-1, keepdims=True))
            log_total = row_max + jnp.log(lax.optimization_barrier(jnp.sum(jnp.exp(scores - row_max), axis=-1, keepdims=True)))
            attn_probs = jnp.exp(scores - log_total).astype(jnp.bfloat16)
            mixed = jnp.dot(attn_probs, value_rows, preferred_element_type=jnp.float32).astype(jnp.bfloat16)
            return (mixed, log_total[:, 0])

        def head_backward(operands):
            query_rows, key_rows, value_rows, grad_heads, log_total = operands
            scores = masked_scores(query_rows, key_rows)
            probs_full = jnp.exp(scores - log_total[:, None])
            probs_half = probs_full.astype(jnp.bfloat16)
            grad_probs = jnp.dot(grad_heads, value_rows.T, preferred_element_type=jnp.float32)
            row_delta = lax.optimization_barrier(jnp.sum(probs_full * grad_probs, axis=-1, keepdims=True))
            grad_scores = (scale_value * probs_full * (grad_probs - row_delta)).astype(jnp.bfloat16)
            grad_query = jnp.dot(grad_scores, key_rows, preferred_element_type=jnp.float32)
            grad_key = jnp.dot(grad_scores.T, query_rows, preferred_element_type=jnp.float32)
            grad_value = jnp.dot(probs_half.T, grad_heads, preferred_element_type=jnp.float32)
            return (grad_query, grad_key, grad_value)
        mixed_heads, log_totals = lax.map(head_forward, (query_all, key_all, value_all))
        mixed_rows = mixed_heads.transpose(1, 0, 2).reshape(length, D)
        attn_out = jnp.dot(mixed_rows, dense_weight, preferred_element_type=jnp.float32) + dense_bias.astype(jnp.float32)
        up_out = jnp.dot(mlp_in, up_weight, preferred_element_type=jnp.float32) + up_bias.astype(jnp.float32)
        activated, gelu_slope = gelu_pair(up_out)
        activated = activated.astype(jnp.bfloat16)
        mlp_out = jnp.dot(activated, down_weight, preferred_element_type=jnp.float32) + down_bias.astype(jnp.float32)
        block_seq = (x_full + attn_out + mlp_out).astype(jnp.bfloat16)
        grad_full = cot_seq.astype(jnp.float32)
        grad_down = jnp.dot(activated.T, cot_seq, preferred_element_type=jnp.float32)
        output_bias_grad = lax.optimization_barrier(jnp.sum(grad_full, axis=0))
        grad_up = jnp.dot(cot_seq, down_weight.T, preferred_element_type=jnp.float32) * gelu_slope
        grad_up_half = grad_up.astype(jnp.bfloat16)
        grad_up_weight = jnp.dot(mlp_in.T, grad_up_half, preferred_element_type=jnp.float32)
        up_bias_grad = lax.optimization_barrier(jnp.sum(grad_up, axis=0))
        grad_mlp_in = jnp.dot(grad_up_half, up_weight.T, preferred_element_type=jnp.float32)
        grad_dense = jnp.dot(mixed_rows.T, cot_seq, preferred_element_type=jnp.float32)
        grad_mixed = jnp.dot(cot_seq, dense_weight.T, preferred_element_type=jnp.float32).astype(jnp.bfloat16)
        grad_mixed = grad_mixed.reshape(length, HEADS, HD).transpose(1, 0, 2)
        grad_query, grad_key, grad_value = lax.map(head_backward, (query_all, key_all, value_all, grad_mixed, log_totals))
        sent_query, sent_key, sent_value = lax.optimization_barrier((grad_query.astype(jnp.bfloat16), grad_key.astype(jnp.bfloat16), grad_value.astype(jnp.bfloat16)))
        sent_query = sent_query.transpose(1, 0, 2).astype(jnp.float32)
        sent_key = sent_key.transpose(1, 0, 2).astype(jnp.float32)
        sent_value = sent_value.transpose(1, 0, 2).astype(jnp.float32)
        grad_joined = jnp.stack([rotate_back(sent_query, cosine, sine_table, ROT), rotate_back(sent_key, cosine, sine_table, ROT), sent_value], axis=2).reshape(length, 3 * D)
        qkv_bias_grad = lax.optimization_barrier(jnp.sum(grad_joined, axis=0))
        grad_joined_half = grad_joined.astype(jnp.bfloat16)
        grad_qkv = jnp.dot(attn_in.T, grad_joined_half, preferred_element_type=jnp.float32)
        grad_attn_in = jnp.dot(grad_joined_half, qkv_weight.T, preferred_element_type=jnp.float32)
        attn_gain_grad = lax.optimization_barrier(jnp.sum(grad_attn_in * normed, axis=0))
        attn_shift_grad = lax.optimization_barrier(jnp.sum(grad_attn_in, axis=0))
        mlp_gain_grad = lax.optimization_barrier(jnp.sum(grad_mlp_in * normed, axis=0))
        mlp_shift_grad = lax.optimization_barrier(jnp.sum(grad_mlp_in, axis=0))
        grad_input = grad_full + norm_backward(grad_attn_in, normed, inv_std, attn_gain) + norm_backward(grad_mlp_in, normed, inv_std, mlp_gain)
        terms = (attn_gain_grad, attn_shift_grad, mlp_gain_grad, mlp_shift_grad, grad_qkv, qkv_bias_grad, grad_dense, output_bias_grad, grad_up_weight, up_bias_grad, grad_down)
        running = tuple((total + term for total, term in zip(running, terms)))
        return (running, (block_seq, grad_input))
    start_totals = (jnp.zeros((D,), jnp.float32), jnp.zeros((D,), jnp.float32), jnp.zeros((D,), jnp.float32), jnp.zeros((D,), jnp.float32), jnp.zeros((D, 3 * D), jnp.float32), jnp.zeros((3 * D,), jnp.float32), jnp.zeros((D, D), jnp.float32), jnp.zeros((D,), jnp.float32), jnp.zeros((D, FF), jnp.float32), jnp.zeros((FF,), jnp.float32), jnp.zeros((FF, D), jnp.float32))
    totals, (block_out, input_grad) = lax.scan(one_sequence, start_totals, (hidden_in, positions, out_cotangent))
    return (block_out, input_grad, totals[0], totals[1], totals[2], totals[3], totals[4], totals[5], totals[6], totals[7], totals[8], totals[9], totals[10], totals[7])
```

```python
import math

import jax
import jax.numpy as jnp
from jax import lax
from jax.sharding import PartitionSpec as P

HEADS = 16
HD = 64
ROT = 16


NORM_EPS = 1e-05
ROPE_BASE = 10000.0
ROOT_HALF = 0.7071067811865476
INV_ROOT_TWO_PI = 0.3989422804014327
MASK_FILL = -1e30


def layer_norm(values):
    row_mean = jnp.mean(values, axis=-1, keepdims=True)
    centered = values - row_mean
    inv_std = lax.rsqrt(jnp.mean(centered * centered, axis=-1, keepdims=True) + NORM_EPS)
    return (centered * inv_std, inv_std)


def affine(normed, norm_gain, norm_shift):
    return normed * norm_gain.astype(jnp.float32) + norm_shift.astype(jnp.float32)


def norm_backward(grad_out, normed, inv_std, norm_gain):
    grad_normed = grad_out * norm_gain.astype(jnp.float32)
    mean_grad = jnp.mean(grad_normed, axis=-1, keepdims=True)
    mean_cross = jnp.mean(grad_normed * normed, axis=-1, keepdims=True)
    return inv_std * (grad_normed - mean_grad - normed * mean_cross)


def gelu_pair(hidden):
    cdf_part = 0.5 * (1.0 + jax.scipy.special.erf(hidden * ROOT_HALF))
    density = jnp.exp(-0.5 * hidden * hidden) * INV_ROOT_TWO_PI
    return (hidden * cdf_part, cdf_part + hidden * density)


def rope_tables(positions, rot_dims):
    half_dims = rot_dims // 2
    inv_freq = jnp.exp(
        jnp.arange(half_dims, dtype=jnp.float32) * (-2.0 * math.log(ROPE_BASE) / rot_dims)
    )
    angles = positions.astype(jnp.float32)[..., None] * inv_freq
    angles = jnp.concatenate([angles, angles], axis=-1)
    return (jnp.cos(angles), jnp.sin(angles))


def rotate(values, cosine, sine_table, rot_dims):
    half_dims = rot_dims // 2
    leading = values[..., :rot_dims]
    turned = jnp.concatenate([-leading[..., half_dims:], leading[..., :half_dims]], axis=-1)
    leading = leading * cosine[..., None, :] + turned * sine_table[..., None, :]
    return jnp.concatenate([leading, values[..., rot_dims:]], axis=-1)


def rotate_back(grad_values, cosine, sine_table, rot_dims):
    half_dims = rot_dims // 2
    leading = grad_values[..., :rot_dims]
    scaled = leading * sine_table[..., None, :]
    leading = leading * cosine[..., None, :] + jnp.concatenate(
        [scaled[..., half_dims:], -scaled[..., :half_dims]], axis=-1
    )
    return jnp.concatenate([leading, grad_values[..., rot_dims:]], axis=-1)


def allowed_block(all_positions, row_start, block_rows, key_len):
    row_index = row_start + jnp.arange(block_rows, dtype=jnp.int32)
    col_index = jnp.arange(key_len, dtype=jnp.int32)
    doc_start = row_index[None, :] - all_positions[:, row_start : row_start + block_rows]
    allowed = (col_index[None, None, :] <= row_index[None, :, None]) & (
        col_index[None, None, :] >= doc_start[:, :, None]
    )
    return allowed[:, None]


def block_scores(
    query_block, key_part, all_positions, row_start, block_rows, row_stop, scale_value
):
    scores = (
        jnp.einsum("sqhd,skhd->shqk", query_block, key_part, preferred_element_type=jnp.float32)
        * scale_value
    )
    return jnp.where(
        allowed_block(all_positions, row_start, block_rows, row_stop), scores, MASK_FILL
    )


def attend_forward(head_side, all_positions):
    seq_count, length, heads_here, packed_width = head_side.shape
    head_dim = packed_width // 3
    query_rows = head_side[..., :head_dim]
    key_rows = head_side[..., head_dim : 2 * head_dim]
    value_rows = head_side[..., 2 * head_dim :]
    block_rows = min(512, length)
    scale_value = 1.0 / math.sqrt(head_dim)
    outputs = []
    totals = []
    for block_index in range(length // block_rows):
        row_start = block_index * block_rows
        row_stop = row_start + block_rows
        scores = block_scores(
            query_rows[:, row_start:row_stop],
            key_rows[:, :row_stop],
            all_positions,
            row_start,
            block_rows,
            row_stop,
            scale_value,
        )
        row_max = jnp.max(scores, axis=-1, keepdims=True)
        log_total = row_max + jnp.log(jnp.sum(jnp.exp(scores - row_max), axis=-1, keepdims=True))
        attn_probs = jnp.exp(scores - log_total).astype(jnp.bfloat16)
        outputs.append(
            jnp.einsum(
                "shqk,skhd->sqhd",
                attn_probs,
                value_rows[:, :row_stop],
                preferred_element_type=jnp.float32,
            ).astype(jnp.bfloat16)
        )
        totals.append(log_total)
    return (jnp.concatenate(outputs, axis=1), jnp.concatenate(totals, axis=2))


def attend_backward(head_side, all_positions, grad_heads, log_total):
    seq_count, length, heads_here, packed_width = head_side.shape
    head_dim = packed_width // 3
    query_rows = head_side[..., :head_dim]
    key_rows = head_side[..., head_dim : 2 * head_dim]
    value_rows = head_side[..., 2 * head_dim :]
    block_rows = min(512, length)
    scale_value = 1.0 / math.sqrt(head_dim)
    query_parts = []
    grad_key_sum = jnp.zeros((seq_count, length, heads_here, head_dim), jnp.float32)
    grad_value_sum = jnp.zeros((seq_count, length, heads_here, head_dim), jnp.float32)
    for block_index in range(length // block_rows):
        row_start = block_index * block_rows
        row_stop = row_start + block_rows
        query_block = query_rows[:, row_start:row_stop]
        key_part = key_rows[:, :row_stop]
        value_part = value_rows[:, :row_stop]
        grad_block = grad_heads[:, row_start:row_stop]
        scores = block_scores(
            query_block, key_part, all_positions, row_start, block_rows, row_stop, scale_value
        )
        probs_full = jnp.exp(scores - log_total[:, :, row_start:row_stop])
        probs_half = probs_full.astype(jnp.bfloat16)
        grad_probs = jnp.einsum(
            "sqhd,skhd->shqk", grad_block, value_part, preferred_element_type=jnp.float32
        )
        row_delta = jnp.sum(probs_full * grad_probs, axis=-1, keepdims=True)
        grad_scores = (scale_value * probs_full * (grad_probs - row_delta)).astype(jnp.bfloat16)
        query_parts.append(
            jnp.einsum("shqk,skhd->sqhd", grad_scores, key_part, preferred_element_type=jnp.float32)
        )
        grad_key_sum = grad_key_sum.at[:, :row_stop].add(
            jnp.einsum(
                "shqk,sqhd->skhd", grad_scores, query_block, preferred_element_type=jnp.float32
            )
        )
        grad_value_sum = grad_value_sum.at[:, :row_stop].add(
            jnp.einsum(
                "shqk,sqhd->skhd", probs_half, grad_block, preferred_element_type=jnp.float32
            )
        )
    grad_query = jnp.concatenate(query_parts, axis=1)
    return jnp.concatenate([grad_query, grad_key_sum, grad_value_sum], axis=-1).astype(jnp.bfloat16)


def gather_rows(piece, axis_name):
    count = lax.axis_size(axis_name)
    copies = jnp.broadcast_to(piece[None], (count,) + piece.shape)
    return lax.all_to_all(copies, axis_name, split_axis=0, concat_axis=0, tiled=True)


def sum_owned(parts, axis_name):
    moved = lax.all_to_all(parts, axis_name, split_axis=0, concat_axis=0, tiled=True)
    return jnp.sum(moved.astype(jnp.float32), axis=0)


def local(
    hidden_in,
    positions,
    out_cotangent,
    attn_gain,
    attn_shift,
    mlp_gain,
    mlp_shift,
    qkv_weight,
    qkv_bias,
    dense_weight,
    dense_bias,
    up_weight,
    up_bias,
    down_weight,
    down_bias,
):
    f32, bf16 = jnp.float32, jnp.bfloat16
    seq_count, local_len, width = hidden_in.shape
    sp_size, fsdp_size = lax.axis_size("sp"), lax.axis_size("fsdp")
    sp_index = lax.axis_index("sp")
    total_len = local_len * sp_size
    rows_all = seq_count * total_len
    own_width = width // fsdp_size
    heads_here = HEADS // sp_size
    qkv_cols = qkv_weight.shape[1] // sp_size
    head_cols = width // sp_size
    ff_all = up_weight.shape[1]
    ff_piece = ff_all // (sp_size * fsdp_size)
    ff_here = ff_piece * fsdp_size
    own_rows = width // (sp_size * fsdp_size)

    x_all = lax.all_gather(hidden_in, "sp", axis=1, tiled=True)
    w_qkv = gather_rows(
        lax.dynamic_slice_in_dim(qkv_weight, sp_index * qkv_cols, qkv_cols, axis=1), "fsdp"
    ).reshape(width, qkv_cols)
    vectors = lax.all_gather(
        jnp.concatenate(
            [attn_gain, attn_shift, mlp_gain, mlp_shift, dense_bias, down_bias, qkv_bias, up_bias]
        ),
        "fsdp", axis=0, tiled=False,
    )
    g_attn, s_attn, g_mlp, s_mlp, b_dense, b_down = (
        vectors[:, k * own_width : (k + 1) * own_width].reshape(width) for k in range(6)
    )
    start = 6 * own_width
    own_qkv = qkv_bias.shape[0]
    b_qkv = lax.dynamic_slice_in_dim(
        vectors[:, start : start + own_qkv].reshape(-1), sp_index * qkv_cols, qkv_cols
    )
    b_up = lax.dynamic_slice_in_dim(
        vectors[:, start + own_qkv :], sp_index * ff_piece, ff_piece, axis=1
    ).reshape(ff_here)
    all_positions = lax.all_gather(positions, "sp", axis=1, tiled=True)
    cot_all = lax.all_gather(out_cotangent, "sp", axis=1, tiled=True)
    w_up = gather_rows(
        lax.dynamic_slice_in_dim(
            up_weight.reshape(own_width, fsdp_size, sp_size, ff_piece), sp_index, 1, axis=2
        ).reshape(own_width, ff_here),
        "fsdp",
    ).reshape(width, ff_here)
    w_down = gather_rows(
        lax.dynamic_slice_in_dim(down_weight, sp_index * ff_piece, ff_piece, axis=0), "fsdp"
    ).reshape(ff_here, width)
    w_dense = lax.dynamic_slice_in_dim(
        gather_rows(dense_weight, "fsdp").reshape(width, width),
        sp_index * head_cols, head_cols, axis=0,
    )

    normed_all, _ = layer_norm(x_all.astype(f32).reshape(rows_all, width))
    attn_in = affine(normed_all, g_attn, s_attn).astype(bf16)
    mlp_in = affine(normed_all, g_mlp, s_mlp).astype(bf16)
    cot_rows = cot_all.reshape(rows_all, width)

    joined = jnp.dot(attn_in, w_qkv, preferred_element_type=f32) + b_qkv.astype(f32)
    joined = joined.reshape(seq_count, total_len, heads_here, 3, HD)
    cosine, sine_table = rope_tables(all_positions, ROT)
    head_side = jnp.concatenate(
        [
            rotate(joined[:, :, :, 0], cosine, sine_table, ROT),
            rotate(joined[:, :, :, 1], cosine, sine_table, ROT),
            joined[:, :, :, 2],
        ],
        axis=-1,
    ).astype(bf16)
    mixed_heads, log_total = attend_forward(head_side, all_positions)
    mixed_rows = mixed_heads.reshape(rows_all, head_cols)
    up_out = jnp.dot(mlp_in, w_up, preferred_element_type=f32) + b_up.astype(f32)
    activated, gelu_slope = gelu_pair(up_out)
    activated = activated.astype(bf16)
    out_part = jnp.dot(mixed_rows, w_dense, preferred_element_type=f32) + jnp.dot(
        activated, w_down, preferred_element_type=f32
    )
    out_part, cot_rows = lax.optimization_barrier((out_part.astype(bf16), cot_rows))
    out_sum = lax.psum_scatter(
        out_part.reshape(seq_count, total_len, width),
        "sp", scatter_dimension=1, tiled=True,
    )
    x_own = hidden_in.astype(f32)
    block_out = (
        x_own + out_sum.astype(f32) + (b_dense.astype(f32) + b_down.astype(f32))
    ).astype(bf16)

    grad_up = jnp.einsum("rd,fd->rf", cot_rows, w_down, preferred_element_type=f32) * gelu_slope
    grad_up_half = grad_up.astype(bf16)
    up_bias_part = jnp.sum(grad_up, axis=0)
    grad_mlp_in = jnp.einsum("rf,df->rd", grad_up_half, w_up, preferred_element_type=f32)
    grad_mixed = jnp.einsum(
        "re,de->rd", cot_rows, w_dense, preferred_element_type=f32
    ).astype(bf16)
    grad_heads = grad_mixed.reshape(seq_count, total_len, heads_here, HD)
    grad_down = jnp.einsum("rf,rd->fd", activated, cot_rows, preferred_element_type=f32)
    grad_dense = jnp.einsum("rd,re->de", mixed_rows, cot_rows, preferred_element_type=f32)
    grad_up_weight = jnp.einsum("rd,rf->df", mlp_in, grad_up_half, preferred_element_type=f32)
    grad_down, grad_dense, grad_up_weight, grad_heads = lax.optimization_barrier(
        (grad_down.astype(bf16), grad_dense.astype(bf16), grad_up_weight.astype(bf16), grad_heads)
    )

    def by_owner(grad, cols):
        return (
            grad.reshape(sp_size, fsdp_size, own_rows, cols)
            .transpose(1, 0, 2, 3)
            .reshape(fsdp_size, sp_size * own_rows, cols)
        )

    down_rows = sum_owned(grad_down.reshape(fsdp_size, ff_piece, width), "fsdp").astype(bf16)
    dense_grad = sum_owned(grad_dense.reshape(fsdp_size, own_rows, width), "fsdp")
    down_grad = lax.ppermute(
        down_rows,
        ("sp", "fsdp"),
        [(s * fsdp_size + f, f * sp_size + s) for s in range(sp_size) for f in range(fsdp_size)],
    ).astype(f32)
    up_rows = sum_owned(by_owner(grad_up_weight, ff_here), "fsdp").astype(bf16)
    up_grad = (
        lax.all_to_all(
            up_rows.reshape(sp_size, own_rows, ff_here),
            "sp", split_axis=0, concat_axis=0, tiled=True,
        )
        .reshape(sp_size, own_rows, fsdp_size, ff_piece)
        .transpose(1, 2, 0, 3)
        .reshape(own_rows, ff_all)
        .astype(f32)
    )
    grad_tokens = attend_backward(head_side, all_positions, grad_heads, log_total).astype(f32)
    grad_joined = jnp.stack(
        [
            rotate_back(grad_tokens[..., :HD], cosine, sine_table, ROT),
            rotate_back(grad_tokens[..., HD : 2 * HD], cosine, sine_table, ROT),
            grad_tokens[..., 2 * HD :],
        ],
        axis=3,
    ).reshape(rows_all, qkv_cols)
    qkv_bias_part = jnp.sum(grad_joined, axis=0)
    grad_joined_half = grad_joined.astype(bf16)
    grad_attn_in = jnp.einsum("rc,dc->rd", grad_joined_half, w_qkv, preferred_element_type=f32)
    normed_part = grad_attn_in * g_attn.astype(f32) + grad_mlp_in * g_mlp.astype(f32)
    grad_normed = lax.psum_scatter(
        normed_part.astype(bf16).reshape(seq_count, total_len, width),
        "sp", scatter_dimension=1, tiled=True,
    ).astype(f32)

    grad_qkv = jnp.einsum(
        "rd,rc->dc", attn_in, grad_joined_half, preferred_element_type=f32
    ).astype(bf16)
    qkv_rows = sum_owned(by_owner(grad_qkv, qkv_cols), "fsdp").astype(bf16)
    qkv_grad = (
        lax.all_to_all(
            qkv_rows.reshape(sp_size, own_rows, qkv_cols),
            "sp", split_axis=0, concat_axis=0, tiled=True,
        )
        .transpose(1, 0, 2)
        .reshape(own_rows, sp_size * qkv_cols)
        .astype(f32)
    )

    owners = sp_size * fsdp_size
    up_bias_full = lax.dynamic_update_slice_in_dim(
        jnp.zeros((fsdp_size, sp_size, ff_piece), f32),
        up_bias_part.reshape(fsdp_size, 1, ff_piece), sp_index, axis=1,
    ).reshape(owners, ff_piece)
    qkv_bias_full = lax.dynamic_update_slice_in_dim(
        jnp.zeros((sp_size * qkv_cols,), f32), qkv_bias_part, sp_index * qkv_cols, axis=0
    ).reshape(owners, -1)
    grad_own = out_cotangent.astype(f32)
    sums = [
        jnp.sum(grad_attn_in * normed_all, axis=0),
        jnp.sum(grad_attn_in, axis=0),
        jnp.sum(grad_mlp_in * normed_all, axis=0),
        jnp.sum(grad_mlp_in, axis=0),
        jnp.sum(grad_own, axis=(0, 1)),
    ]
    vector_parts = jnp.concatenate(
        [up_bias_full, qkv_bias_full] + [v.reshape(owners, own_rows) for v in sums], axis=1
    )
    vector_sums = sum_owned(
        sum_owned(vector_parts.reshape(sp_size, fsdp_size, -1), "sp"), "fsdp"
    )
    qkv_piece = qkv_cols // fsdp_size
    up_bias_grad = vector_sums[:ff_piece]
    qkv_bias_grad = vector_sums[ff_piece : ff_piece + qkv_piece]
    tail = vector_sums[ff_piece + qkv_piece :]
    attn_gain_grad, attn_shift_grad, mlp_gain_grad, mlp_shift_grad, output_bias_grad = (
        tail[k * own_rows : (k + 1) * own_rows] for k in range(5)
    )

    normed_own, inv_std = layer_norm(x_own)
    mean_grad = jnp.mean(grad_normed, axis=-1, keepdims=True)
    mean_cross = jnp.mean(grad_normed * normed_own, axis=-1, keepdims=True)
    input_grad = grad_own + inv_std * (grad_normed - mean_grad - normed_own * mean_cross)
    return (
        block_out,
        input_grad,
        attn_gain_grad,
        attn_shift_grad,
        mlp_gain_grad,
        mlp_shift_grad,
        qkv_grad,
        qkv_bias_grad,
        dense_grad,
        output_bias_grad,
        up_grad,
        up_bias_grad,
        down_grad,
        output_bias_grad,
    )


def solution(mesh):
    placed = (
        P("fsdp", "sp", None),
        P("fsdp", "sp"),
        P("fsdp", "sp", None),
        P("fsdp"),
        P("fsdp"),
        P("fsdp"),
        P("fsdp"),
        P("fsdp", None),
        P("fsdp"),
        P("fsdp", None),
        P("fsdp"),
        P("fsdp", None),
        P("fsdp"),
        P("fsdp", None),
        P("fsdp"),
    )
    return jax.shard_map(
        local,
        mesh=mesh,
        in_specs=placed,
        out_specs=(
            P("fsdp", "sp", None),
            P("fsdp", "sp", None),
            P(("sp", "fsdp")),
            P(("sp", "fsdp")),
            P(("sp", "fsdp")),
            P(("sp", "fsdp")),
            P(("sp", "fsdp"), None),
            P(("sp", "fsdp")),
            P(("sp", "fsdp"), None),
            P(("sp", "fsdp")),
            P(("sp", "fsdp"), None),
            P(("sp", "fsdp")),
            P(("sp", "fsdp"), None),
            P(("sp", "fsdp")),
        ),
        check_vma=False,
    )
```
